256 devices in a mesh: fx: 32 (over z, x), fy: 8 (over y, core).
Axes of the slice: x: 4, y: 4, z: 8, core: 2. Of those that a mesh axis runs over, the one named last changes fastest.
Arguments:
- right_side: float32 [4096, 2048], P(('fx', 'fy'))
- coupling: float32 [4096, 11, 4096], P(('fx', 'fy')), may hold values from -0.109375 to 0.109375
- face_columns: int32 [4096, 11], P(('fx', 'fy')), may hold values from 0 to 31, as said below
- ghost_lists: int32 [1024, 4], P(('fx', 'fy')), may hold values from 0 to 15, as said below
Outputs:
- solution: float32 [4096, 2048], P(('fx', 'fy'))
- residual: float32 [4096, 2048], P(('fx', 'fy'))
The draws below stay inside these ranges and needn't reach their ends.
Inputs may be any that keep to these rules, and one draw needn't show every extreme that they name: face_columns[f, 0] is f's own index within its block; entries 1 to 6 name other faces of the same block, all distinct and below 16; entries 7 to 10 are distinct and name received faces, 16 + d * 4 + g for the g-th face of group d of the extended list; every received slot of every block is named by some row of that block. `ghost_lists`: each row names 4 distinct faces of its block by local index.
All inputs are finite; a program needn't handle non-finite values.
Results may differ from the reference program's by a relative error of at most 0.0003.
Values sent between devices are 32-bit elements; how exact they have to be, the bound alone decides.
No kernel may reach another device: no remote copies, remote signals or barrier semaphores. Data moves between devices by JAX's collectives and lax.ppermute only.
A program may use at most 64 MiB of HBM per device.

```python
import jax
import jax.numpy as jnp
from jax import lax

DOF = 64
NRHS = 32
BLOCKS = 11
OWNED = 7
POWERS = 3
FACE_DEV = 16
GHOST = 4
FACES = 4096
N_FX = 32
N_FY = 8


def draw_right_side(key, part):
    keys = jax.random.split(key, 3)
    blocks_total = N_FX * N_FY
    block_id = (jnp.arange(FACES) // FACE_DEV).astype(jnp.float32)
    position = block_id / max(blocks_total - 1, 1) - 0.5
    base = jax.random.normal(keys[0], (FACES, DOF * NRHS), jnp.float32)
    ramp = jnp.exp(position * jnp.log(3.0))
    face_scale = jnp.exp(jax.random.uniform(keys[1], (FACES,), jnp.float32, jnp.log(0.3), jnp.log(3.0)))
    column_scale = jnp.exp(jax.random.uniform(keys[2], (NRHS,), jnp.float32, jnp.log(0.3), jnp.log(3.0)))
    column_scale = jnp.tile(column_scale, DOF)
    return base * (ramp * face_scale)[:, None] * column_scale[None, :]


def draw_face_columns(key, part):
    keys = jax.random.split(key, 3)
    blocks_total = N_FX * N_FY
    local = jnp.arange(FACES) % FACE_DEV
    row_keys = jax.random.split(keys[0], FACES)

    def owned_pick(one_key):
        return jax.random.permutation(one_key, FACE_DEV - 1)[:OWNED - 1]
    owned = jax.vmap(owned_pick)(row_keys)
    owned = owned + (owned >= local[:, None]).astype(owned.dtype)
    block_keys = jax.random.split(keys[1], blocks_total)

    def cover_pick(one_key):
        return jax.random.permutation(one_key, FACE_DEV)
    cover = jax.vmap(cover_pick)(block_keys).reshape(FACES) % (4 * GHOST)
    other_keys = jax.random.split(keys[2], FACES)

    def other_pick(one_key):
        return jax.random.permutation(one_key, 4 * GHOST - 1)[:BLOCKS - OWNED - 1]
    others = jax.vmap(other_pick)(other_keys)
    others = others + (others >= cover[:, None]).astype(others.dtype)
    received = jnp.concatenate([others, cover[:, None]], axis=1) + FACE_DEV
    return jnp.concatenate([local[:, None], owned, received], axis=1).astype(jnp.int32)


def draw_ghost_lists(key, part):
    list_keys = jax.random.split(key, 4 * N_FX * N_FY)

    def list_pick(one_key):
        return jax.random.permutation(one_key, FACE_DEV)[:GHOST]
    return jax.vmap(list_pick)(list_keys).astype(jnp.int32)


def level_of(own_key, shape, pieces, least, largest):
    def one(dim, blocks):
        draws = jax.random.uniform(jax.random.fold_in(jax.random.fold_in(own_key, 6), dim), (blocks,), jnp.float32, least / len(pieces), largest / len(pieces))
        return jnp.repeat(jnp.exp(draws), shape[dim] // blocks).reshape((-1,) + (1,) * (len(shape) - dim - 1))

    level = one(*pieces[0])
    for cut in pieces[1:]:
        level = level * one(*cut)
    return level


def centred(key, dims, deviation, limit, cuts=(), held_as=jnp.bfloat16):
    array = deviation * jax.random.normal(key, dims, jnp.float32)
    if cuts:
        array = array * level_of(key, dims, cuts, -0.22, 0.18)
    return jnp.clip(array, -limit, limit).astype(held_as)


def setup_inputs(seed: int = 0) -> dict:
    seeds = jax.random.split(jax.random.key(seed), 5)
    return {
        "right_side": draw_right_side(jax.random.fold_in(seeds[4], 71), 0),
        "coupling": centred(seeds[1], (FACES, BLOCKS, DOF * DOF), (4 * BLOCKS * DOF) ** -0.5, 0.109375, ((0, 256),), jnp.float32),
        "face_columns": draw_face_columns(jax.random.fold_in(seeds[4], 71), 0),
        "ghost_lists": draw_ghost_lists(jax.random.fold_in(seeds[4], 71), 0),
    }


def extended_grid(field, ghost_lists):
    width = field.shape[1]
    field_grid = field.reshape(N_FX, N_FY, FACE_DEV, width)
    lists = ghost_lists.reshape(N_FX, N_FY, 4, GHOST)

    def select_rows(direction):
        return jnp.take_along_axis(field_grid, lists[:, :, direction, :][..., None], axis=2)
    zero_fx = jnp.zeros((1, N_FY, GHOST, width), jnp.float32)
    zero_fy = jnp.zeros((N_FX, 1, GHOST, width), jnp.float32)
    from_lower_x = jnp.concatenate([zero_fx, select_rows(1)[:-1]], axis=0)
    from_upper_x = jnp.concatenate([select_rows(0)[1:], zero_fx], axis=0)
    from_lower_y = jnp.concatenate([zero_fy, select_rows(3)[:, :-1]], axis=1)
    from_upper_y = jnp.concatenate([select_rows(2)[:, 1:], zero_fy], axis=1)
    return jnp.concatenate([field_grid, from_lower_x, from_upper_x, from_lower_y, from_upper_y], axis=2)

def apply_coupling(field, coupling, face_columns, ghost_lists):
    extended = extended_grid(field, ghost_lists)
    column_grid = face_columns.reshape(N_FX, N_FY, FACE_DEV * BLOCKS)
    block_mats = coupling.reshape(N_FX, N_FY, FACE_DEV, BLOCKS, DOF, DOF)

    def one_row(items):
        ext_row, col_row, mat_row = items
        picked = jnp.take_along_axis(ext_row, col_row[..., None], axis=1)
        picked = picked.reshape(N_FY, FACE_DEV, BLOCKS, DOF, NRHS)
        return jnp.einsum('yfkab,yfkbr->yfar', mat_row, picked, precision=lax.Precision.HIGHEST)
    result = lax.map(one_row, (extended, column_grid, block_mats))
    return result.reshape(FACES, DOF * NRHS)

def solve_small(gram_total):
    count = NRHS
    row_ids = jnp.arange((POWERS + 1) * count)[:, None]
    col_ids = jnp.arange(POWERS * count)[None, :]
    shift_map = ((row_ids == col_ids) | (row_ids == col_ids + count)).astype(jnp.float32)
    first = (row_ids == jnp.arange(count)[None, :]).astype(jnp.float32)
    high = lax.Precision.HIGHEST
    normal_matrix = jnp.dot(shift_map.T, jnp.dot(gram_total, shift_map, precision=high), precision=high)
    right_terms = jnp.dot(shift_map.T, gram_total[:, :count], precision=high)
    factor = jnp.linalg.cholesky(normal_matrix)
    coeffs = jax.scipy.linalg.cho_solve((factor, True), right_terms)
    combo = first - jnp.dot(shift_map, coeffs, precision=high)
    return (coeffs, combo)

def reference(right_side, coupling, face_columns, ghost_lists):
    fields = [right_side]
    for power_index in range(POWERS):
        fields.append(apply_coupling(fields[-1], coupling, face_columns, ghost_lists))
    stacked = jnp.concatenate([item.reshape(FACES * DOF, NRHS) for item in fields], axis=1)
    high = lax.Precision.HIGHEST
    gram_total = jnp.dot(stacked.T.astype(jnp.float32), stacked.astype(jnp.float32), precision=high, preferred_element_type=jnp.float32)
    coeffs, combo = solve_small(gram_total)
    solution = jnp.dot(stacked[:, :POWERS * NRHS], coeffs, precision=high)
    residual = jnp.dot(stacked, combo, precision=high)
    return (solution.reshape(FACES, DOF * NRHS), residual.reshape(FACES, DOF * NRHS))
```

```python
import jax
import jax.numpy as jnp
from jax import lax
from jax.sharding import PartitionSpec as P

DOF = 64
NRHS = 32
BLOCKS = 11
POWERS = 3


def from_behind(block, axis, distance):
    devices = range(lax.axis_size(axis))
    route = [(i - distance, i) for i in devices if i - distance in devices]
    return lax.ppermute(block, axis, route)


def receive_rows(field, ghost_lists):
    from_lower_x = from_behind(jnp.take(field, ghost_lists[1], axis=0), "fx", 1)
    from_upper_x = from_behind(jnp.take(field, ghost_lists[0], axis=0), "fx", -1)
    from_lower_y = from_behind(jnp.take(field, ghost_lists[3], axis=0), "fy", 1)
    from_upper_y = from_behind(jnp.take(field, ghost_lists[2], axis=0), "fy", -1)
    return jnp.concatenate([from_lower_x, from_upper_x, from_lower_y, from_upper_y], axis=0)


def contract(block_mats, picked):
    face_count = picked.shape[0]
    shaped = picked.reshape(face_count, picked.shape[1], DOF, NRHS)
    result = jnp.einsum("fkab,fkbr->far", block_mats, shaped, precision=lax.Precision.HIGHEST)
    return result.reshape(face_count, DOF * NRHS)


def solve_small(gram_total):
    count = NRHS
    row_ids = jnp.arange((POWERS + 1) * count)[:, None]
    col_ids = jnp.arange(POWERS * count)[None, :]
    shift_map = ((row_ids == col_ids) | (row_ids == col_ids + count)).astype(jnp.float32)
    first = (row_ids == jnp.arange(count)[None, :]).astype(jnp.float32)
    high = lax.Precision.HIGHEST
    normal_matrix = jnp.dot(
        shift_map.T, jnp.dot(gram_total, shift_map, precision=high), precision=high
    )
    right_terms = jnp.dot(shift_map.T, gram_total[:, :count], precision=high)
    factor = jnp.linalg.cholesky(normal_matrix)
    coeffs = jax.scipy.linalg.cho_solve((factor, True), right_terms)
    combo = first - jnp.dot(shift_map, coeffs, precision=high)
    return (coeffs, combo)


def pack_gram(gram):
    tail = gram[64:96, 64:128]
    return jnp.concatenate(
        [
            gram[:32],
            jnp.concatenate([gram[32:64, 32:], gram[96:, 96:]], axis=1),
            jnp.concatenate([tail[:16], tail[16:]], axis=1),
        ],
        axis=0,
    )


def unpack_gram(packed):
    tail = jnp.concatenate([packed[64:, :64], packed[64:, 64:]], axis=0)
    row0 = packed[:32]
    row1 = packed[32:64, :96]
    last = packed[32:64, 96:]
    row1 = jnp.concatenate([row0[:, 32:64].T, row1], axis=1)
    row2 = jnp.concatenate([row0[:, 64:96].T, row1[:, 64:96].T, tail], axis=1)
    row3 = jnp.concatenate([row0[:, 96:].T, row1[:, 96:].T, tail[:, 32:].T, last], axis=1)
    return jnp.concatenate([row0, row1, row2, row3], axis=0)


ROUNDS = (("fy", (1, 2, 3)), ("fy", (4,)), ("fx", (1, 2, 3)), ("fx", (4, 8, 12)), ("fx", (16,)))


def add_over_devices(part):
    for axis, offsets in ROUNDS:
        devices = range(lax.axis_size(axis))
        others = [lax.ppermute(part, axis, [(i, i ^ d) for i in devices]) for d in offsets]
        for other in others:
            part = part + other
    return part


def on_device(right_side, coupling, face_columns, ghost_lists):
    face_count = right_side.shape[0]
    block_mats = coupling.reshape(face_count, BLOCKS, DOF, DOF)
    high = lax.Precision.HIGHEST

    def as_rows(field):
        return field.reshape(face_count * DOF, NRHS)

    fields = [right_side]
    for power_index in range(POWERS):
        power_field = fields[-1]
        received = receive_rows(power_field, ghost_lists)
        extended = jnp.concatenate([power_field, received], axis=0)
        fields.append(contract(block_mats, jnp.take(extended, face_columns, axis=0)))
    stacked = jnp.concatenate([as_rows(item) for item in fields], axis=1)
    local_gram = jnp.dot(stacked.T, stacked, precision=high, preferred_element_type=jnp.float32)
    gram_total = unpack_gram(add_over_devices(pack_gram(local_gram)))
    coeffs, combo = solve_small(gram_total)
    solution = jnp.dot(stacked[:, : POWERS * NRHS], coeffs, precision=high)
    residual = jnp.dot(stacked, combo, precision=high)
    return (solution.reshape(face_count, DOF * NRHS), residual.reshape(face_count, DOF * NRHS))


def solution(mesh):
    placed = (
        P(("fx", "fy"), None),
        P(("fx", "fy"), None, None),
        P(("fx", "fy"), None),
        P(("fx", "fy"), None),
    )
    return jax.shard_map(
        on_device,
        mesh=mesh,
        in_specs=placed,
        out_specs=(P(("fx", "fy"), None), P(("fx", "fy"), None)),
        check_vma=False,
    )
```

```python
import functools

import jax
import jax.numpy as jnp
from jax import lax
from jax.experimental import pallas as pl
from jax.experimental.pallas import tpu as pltpu
from jax.sharding import PartitionSpec as P

DOF = 64
NRHS = 32
BLOCKS = 11
OWNED = 7
POWERS = 3
FACE_DEV = 16
GHOST = 4
LANES = 128
COPIES = LANES // NRHS
ROWS = FACE_DEV * DOF
OWN_DEPTH = 512
GHOST_DEPTH = 256
SYSTEM = POWERS * NRHS

VMEM = pl.BlockSpec(memory_space=pltpu.VMEM)
SMEM = pl.BlockSpec(memory_space=pltpu.SMEM)
F32 = jnp.float32
BF16 = jnp.bfloat16


def shape_of(rows, columns, dtype=F32):
    return jax.ShapeDtypeStruct((rows, columns), dtype)


def lane_group(rows):
    return lax.broadcasted_iota(jnp.int32, (rows, LANES), 1) // NRHS


def by_group(group, parts):
    low = jnp.where(group == 0, parts[0], parts[1])
    high = jnp.where(group == 2, parts[2], parts[3])
    return jnp.where(group < 2, low, high)


def spread(tile):
    group = lane_group(tile.shape[0])
    turned = [tile] + [pltpu.roll(tile, NRHS * s, 1) for s in range(1, COPIES)]
    return [by_group(group, [turned[(c - j) % COPIES] for c in range(COPIES)]) for j in range(COPIES)]


def high_low(field):
    group = lane_group(field.shape[0])
    high = field.astype(BF16).astype(F32)
    return jnp.where(group % 2 == 0, high, field - high).astype(BF16)


def first_directions():
    odd_x = lax.rem(lax.axis_index("fx"), 2)
    odd_y = lax.rem(lax.axis_index("fy"), 2)
    return (1 - odd_x, odd_x, 3 - odd_y, 2 + odd_y)


def inside(direction):
    fx, fy = lax.axis_index("fx"), lax.axis_index("fy")
    last_x, last_y = lax.axis_size("fx") - 1, lax.axis_size("fy") - 1
    out = (direction == 0) & (fx == 0) | (direction == 1) & (fx == last_x)
    return jnp.logical_not(out | (direction == 2) & (fy == 0) | (direction == 3) & (fy == last_y))


def write_sends(lists, field_ref, send_refs):
    group = lane_group(FACE_DEV)
    for direction, send_ref in zip(first_directions(), send_refs):
        for g in range(GHOST):
            start = lists[direction, g] * DOF
            parts = [field_ref[pl.ds(start + j, FACE_DEV, stride=COPIES), :] for j in range(COPIES)]
            send_ref[g * FACE_DEV : (g + 1) * FACE_DEV, :] = by_group(group, parts)


def spread_kernel(lists, right_ref, field_ref, *send_refs):
    for t in range(DOF // COPIES):
        parts = spread(right_ref[:, t * LANES : (t + 1) * LANES])
        for j in range(COPIES):
            field_ref[pl.ds(COPIES * t + j, FACE_DEV, stride=DOF), :] = parts[j]
    write_sends(lists, field_ref, send_refs)


def weights_kernel(coupling_ref, own_high, own_low, ghost_high, ghost_low):
    rows = own_high.shape[2]
    left = lax.broadcasted_iota(jnp.int32, (rows, LANES), 1) < DOF
    zero = jnp.zeros((rows, LANES), F32)
    order = list(range(OWNED)) + [None] + list(range(OWNED, BLOCKS))
    for face in range(own_high.shape[0]):
        tiles = [zero if k is None else coupling_ref[k, pl.ds(face, rows, stride=8), :] for k in order]
        turned = [zero if k is None else pltpu.roll(tile, DOF, 1) for k, tile in zip(order, tiles)]
        for q in range(len(order) // 2):
            even = jnp.where(left, tiles[2 * q], turned[2 * q + 1])
            odd = jnp.where(left, turned[2 * q], tiles[2 * q + 1])
            if q < OWN_DEPTH // LANES:
                high_ref, low_ref, lane = own_high, own_low, q * LANES
            else:
                high_ref, low_ref, lane = ghost_high, ghost_low, q * LANES - OWN_DEPTH
            for s, part in ((0, even), (1, odd)):
                high = part.astype(BF16)
                high_ref[face, s, :, lane : lane + LANES] = high
                low_ref[face, s, :, lane : lane + LANES] = (part - high.astype(F32)).astype(BF16)


def product(high_ref, low_ref, face, picked):
    depth = picked.shape[0]
    high = high_ref[face].reshape(DOF, depth)
    low = low_ref[face].reshape(DOF, depth)
    both = jnp.dot(high, picked, preferred_element_type=F32)
    both = both + jnp.dot(low, picked, preferred_element_type=F32)
    return both + pltpu.roll(both, NRHS, 1)


def pick(rows_ref, numbers):
    starts = [pl.multiple_of(number * DOF, DOF) for number in numbers]
    return jnp.concatenate([rows_ref[pl.ds(start, DOF), :] for start in starts], axis=0)


def own_kernel(columns, field_ref, high_ref, low_ref, sum_ref, split_ref):
    for face in range(FACE_DEV):
        at = slice(face * DOF, (face + 1) * DOF)
        split_ref[at, :] = high_low(field_ref[at, :])
    for face in range(FACE_DEV):
        numbers = [columns[face, k] for k in range(OWNED)]
        picked = pick(split_ref, numbers + numbers[:1])
        sum_ref[face * DOF : (face + 1) * DOF, :] = product(high_ref, low_ref, face, picked)


def add_ghosts(columns, received, sum_ref, high_ref, low_ref, field_ref, spread_ref, split_ref):
    for direction, received_ref in zip(first_directions(), received):
        keep = inside(direction)
        for g in range(GHOST):
            tile = received_ref[g * FACE_DEV : (g + 1) * FACE_DEV, :]
            parts = spread(jnp.where(keep, tile, 0.0))
            start = (direction * GHOST + g) * DOF
            for j in range(COPIES):
                spread_ref[pl.ds(start + j, FACE_DEV, stride=COPIES), :] = parts[j]
    for slot in range(4 * GHOST):
        at = slice(slot * DOF, (slot + 1) * DOF)
        split_ref[at, :] = high_low(spread_ref[at, :])
    for face in range(FACE_DEV):
        picked = pick(split_ref, [columns[face, k] - FACE_DEV for k in range(OWNED, BLOCKS)])
        total = sum_ref[face * DOF : (face + 1) * DOF, :] + product(high_ref, low_ref, face, picked)
        for s in range(2):
            rows = pl.ds(face * DOF + s, DOF // 2, stride=2)
            field_ref[rows, :] = total[s * DOF // 2 : (s + 1) * DOF // 2, :]


def ghost_kernel(columns, lists, r0, r1, r2, r3, sum_ref, high_ref, low_ref, field_ref, s0, s1, s2, s3, spread_ref, split_ref):
    add_ghosts(columns, (r0, r1, r2, r3), sum_ref, high_ref, low_ref, field_ref, spread_ref, split_ref)
    write_sends(lists, field_ref, (s0, s1, s2, s3))


def last_kernel(
    columns, r0, r1, r2, r3, sum_ref, high_ref, low_ref, f0, f1, f2, system_ref, basis_ref, f3, spread_ref, split_ref
):
    add_ghosts(columns, (r0, r1, r2, r3), sum_ref, high_ref, low_ref, f3, spread_ref, split_ref)
    group = lane_group(LANES)
    gram = jnp.zeros((LANES, 2 * LANES), F32)
    for part in range(ROWS // LANES):
        at = slice(part * LANES, (part + 1) * LANES)
        basis = by_group(group, [ref[at, :] for ref in (f0, f1, f2, f3)])
        high = basis.astype(BF16)
        low = (basis - high.astype(F32)).astype(BF16)
        both = jnp.concatenate([high, low], axis=1)
        basis_ref[at, :] = both
        gram = gram + lax.dot_general(high, both, (((0,), (0,)), ((), ())), preferred_element_type=F32)
    cross = gram[:, LANES:]
    full = gram[:, :LANES] + cross + cross.T
    pairs = full[:SYSTEM] + full[NRHS:]
    lane = lax.broadcasted_iota(jnp.int32, (SYSTEM, LANES), 1)
    system_ref[...] = pltpu.roll(pairs, SYSTEM, 1) + jnp.where(lane < SYSTEM, pairs, 0.0)


def finish_kernel(mine, other, basis_ref, solution_ref, residual_ref, out_ref):
    system = mine[...] + other[...]
    row = lax.broadcasted_iota(jnp.int32, (SYSTEM, LANES), 0)
    for j in range(SYSTEM):
        line = system[j : j + 1, :]
        line = line / line[:, j : j + 1]
        factor = jnp.where(row == j, 0.0, system[:, j : j + 1])
        system = jnp.where(row == j, line, system) - factor * line
    lane = lax.broadcasted_iota(jnp.int32, (SYSTEM, LANES), 1)
    coeffs = jnp.where(lane >= SYSTEM, system, 0.0)
    coeffs = coeffs + pltpu.roll(coeffs, NRHS, 1)
    coeffs = coeffs + pltpu.roll(coeffs, 2 * NRHS, 1)
    zero = jnp.zeros((NRHS, LANES), F32)
    first_row = lax.broadcasted_iota(jnp.int32, (LANES, LANES), 0)
    first_lane = lax.broadcasted_iota(jnp.int32, (LANES, LANES), 1)
    first = jnp.where(first_row == first_lane % NRHS, 1.0, 0.0)
    padded = jnp.concatenate([coeffs, zero], axis=0)
    combo = first - (padded + jnp.concatenate([zero, coeffs], axis=0))
    both = jnp.concatenate([padded, combo], axis=1)
    high = both.astype(BF16)
    low = (both - high.astype(F32)).astype(BF16)
    twice = jnp.concatenate([high, high], axis=0)
    for part in range(ROWS // LANES):
        at = slice(part * LANES, (part + 1) * LANES)
        out = jnp.dot(basis_ref[at, :], twice, preferred_element_type=F32)
        out = out + jnp.dot(basis_ref[at, :LANES], low, preferred_element_type=F32)
        out_ref[0, at, :] = out[:, :LANES]
        out_ref[1, at, :] = out[:, LANES:]
    group = lane_group(FACE_DEV)
    for t in range(DOF // COPIES):
        for side, result_ref in ((0, solution_ref), (1, residual_ref)):
            parts = [out_ref[side, pl.ds(COPIES * t + j, FACE_DEV, stride=DOF), :] for j in range(COPIES)]
            result_ref[:, t * LANES : (t + 1) * LANES] = by_group(group, parts)


def pairs_of(size, second):
    if not second:
        return [(i, i ^ 1) for i in range(size)]
    ahead = [(i, (i + 1) % size) for i in range(1, size, 2)]
    return ahead + [(b, a) for a, b in ahead]


def exchange(sends):
    routes = (("fx", False), ("fx", True), ("fy", False), ("fy", True))
    return [
        lax.ppermute(send, axis, pairs_of(lax.axis_size(axis), second))
        for send, (axis, second) in zip(sends, routes)
    ]


ROUNDS = (("fy", (1,)), ("fy", (2, 4, 6)), ("fx", (1, 2, 3)), ("fx", (4, 8, 12)))
LAST_ROUND = ("fx", 16)


def from_partner(part, axis, distance):
    return lax.ppermute(part, axis, [(i, i ^ distance) for i in range(lax.axis_size(axis))])


def add_over_devices(part):
    for axis, distances in ROUNDS:
        others = [from_partner(part, axis, d) for d in distances]
        part = part + others[0]
        if len(others) == 3:
            part = part + (others[1] + others[2])
    return part, from_partner(part, *LAST_ROUND)


def params(**extra):
    return dict(compiler_params=pltpu.CompilerParams(vmem_limit_bytes=40 << 20, **extra))


def on_device(right_side, coupling, face_columns, ghost_lists):
    send = shape_of(GHOST * FACE_DEV, LANES)
    field_shape = shape_of(ROWS, LANES)
    outs = pl.pallas_call(
        spread_kernel,
        out_shape=[field_shape] + [send] * 4,
        in_specs=[SMEM, VMEM],
        out_specs=[VMEM] * 5,
        name="spread",
        **params(),
    )(ghost_lists, right_side)
    fields, sends = [outs[0]], outs[1:]

    tiles = jnp.transpose(coupling, (1, 0, 2)).reshape(BLOCKS, 2, 8, DOF // 2, LANES)
    tiles = jnp.transpose(tiles, (0, 1, 3, 2, 4)).reshape(BLOCKS, 4 * LANES, LANES)
    halves = 2
    block = DOF // 2 // halves
    own_shape = jax.ShapeDtypeStruct((FACE_DEV, 2, DOF // 2, OWN_DEPTH), BF16)
    ghost_shape = jax.ShapeDtypeStruct((FACE_DEV, 2, DOF // 2, GHOST_DEPTH), BF16)
    place = lambda depth: pl.BlockSpec((8, 2, block, depth), lambda i: (i // halves, 0, i % halves, 0))
    own_high, own_low, ghost_high, ghost_low = pl.pallas_call(
        weights_kernel,
        grid=(2 * halves,),
        out_shape=[own_shape, own_shape, ghost_shape, ghost_shape],
        in_specs=[pl.BlockSpec((BLOCKS, 8 * block, LANES), lambda i: (0, i, 0))],
        out_specs=[place(OWN_DEPTH), place(OWN_DEPTH), place(GHOST_DEPTH), place(GHOST_DEPTH)],
        cost_estimate=pl.CostEstimate(flops=0, transcendentals=0, bytes_accessed=6 << 20),
        name="weights",
        **params(),
    )(tiles)

    own_call = pl.pallas_call(
        own_kernel,
        out_shape=field_shape,
        in_specs=[SMEM, VMEM, VMEM, VMEM],
        out_specs=VMEM,
        scratch_shapes=[pltpu.VMEM((ROWS, LANES), BF16)],
        cost_estimate=pl.CostEstimate(flops=1 << 30, transcendentals=0, bytes_accessed=3 << 20),
        name="own",
        **params(),
    )
    scratch = [pltpu.VMEM((4 * GHOST * DOF, LANES), F32), pltpu.VMEM((4 * GHOST * DOF, LANES), BF16)]
    ghost_call = pl.pallas_call(
        ghost_kernel,
        out_shape=[field_shape] + [send] * 4,
        in_specs=[SMEM, SMEM] + [VMEM] * 7,
        out_specs=[VMEM] * 5,
        scratch_shapes=scratch,
        name="ghost",
        **params(),
    )
    last_call = pl.pallas_call(
        last_kernel,
        out_shape=[shape_of(SYSTEM, LANES), shape_of(ROWS, 2 * LANES, BF16)],
        in_specs=[SMEM] + [VMEM] * 10,
        out_specs=[VMEM] * 2,
        scratch_shapes=[pltpu.VMEM((ROWS, LANES), F32)] + scratch,
        name="last",
        **params(),
    )
    for power in range(POWERS):
        received = exchange(sends)
        own_sum = own_call(face_columns, fields[-1], own_high, own_low)
        if power < POWERS - 1:
            outs = ghost_call(face_columns, ghost_lists, *received, own_sum, ghost_high, ghost_low)
            fields.append(outs[0])
            sends = outs[1:]
        else:
            system, basis = last_call(face_columns, *received, own_sum, ghost_high, ghost_low, *fields)
    mine, other = add_over_devices(system)
    result = shape_of(FACE_DEV, DOF * NRHS)
    return tuple(
        pl.pallas_call(
            finish_kernel,
            out_shape=[result, result],
            in_specs=[VMEM] * 3,
            out_specs=[VMEM] * 2,
            scratch_shapes=[pltpu.VMEM((2, ROWS, LANES), F32)],
            name="finish",
            **params(),
        )(mine, other, basis)
    )


def solution(mesh):
    placed = (
        P(("fx", "fy"), None),
        P(("fx", "fy"), None, None),
        P(("fx", "fy"), None),
        P(("fx", "fy"), None),
    )
    return jax.shard_map(
        on_device,
        mesh=mesh,
        in_specs=placed,
        out_specs=(P(("fx", "fy"), None), P(("fx", "fy"), None)),
        check_vma=False,
    )
```

```python
import functools

import jax
import jax.numpy as jnp
from jax import lax
from jax.experimental import pallas as pl
from jax.experimental.pallas import tpu as pltpu
from jax.sharding import PartitionSpec as P

DOF = 64
NRHS = 32
BLOCKS = 11
OWNED = 7
POWERS = 3
FACE_DEV = 16
GHOST = 4
LANES = 128
COPIES = LANES // NRHS
ROWS = FACE_DEV * DOF
OWN_DEPTH = 512
GHOST_DEPTH = 256
SYSTEM = POWERS * NRHS
CHUNKS = 4
PIVOTS = 8

VMEM = pl.BlockSpec(memory_space=pltpu.VMEM)
ANY = pl.BlockSpec(memory_space=pl.ANY)
SMEM = pl.BlockSpec(memory_space=pltpu.SMEM)
HBM = pl.BlockSpec(memory_space=pltpu.HBM)
F32 = jnp.float32
BF16 = jnp.bfloat16


def shape_of(rows, columns, dtype=F32):
    return jax.ShapeDtypeStruct((rows, columns), dtype)


def lane_group(rows):
    return lax.broadcasted_iota(jnp.int32, (rows, LANES), 1) // NRHS


def by_group(group, parts):
    low = jnp.where(group == 0, parts[0], parts[1])
    high = jnp.where(group == 2, parts[2], parts[3])
    return jnp.where(group < 2, low, high)


def spread(tile):
    group = lane_group(tile.shape[0])
    turned = [tile] + [pltpu.roll(tile, NRHS * s, 1) for s in range(1, COPIES)]
    return [by_group(group, [turned[(c - j) % COPIES] for c in range(COPIES)]) for j in range(COPIES)]


def high_low(field):
    group = lane_group(field.shape[0])
    high = field.astype(BF16).astype(F32)
    return jnp.where(group % 2 == 0, high, field - high).astype(BF16)


def first_directions():
    odd_x = lax.rem(lax.axis_index("fx"), 2)
    odd_y = lax.rem(lax.axis_index("fy"), 2)
    return (odd_x, 1 - odd_x, 2 + odd_y, 3 - odd_y)


def inside(direction):
    fx, fy = lax.axis_index("fx"), lax.axis_index("fy")
    last_x, last_y = lax.axis_size("fx") - 1, lax.axis_size("fy") - 1
    out = (direction == 0) & (fx == 0) | (direction == 1) & (fx == last_x)
    return jnp.logical_not(out | (direction == 2) & (fy == 0) | (direction == 3) & (fy == last_y))


def write_sends(lists, field_ref, send_refs):
    group = lane_group(FACE_DEV)
    for direction, send_ref in zip(first_directions(), send_refs):
        for g in range(GHOST):
            start = lists[direction, g] * DOF
            parts = [field_ref[pl.ds(start + j, FACE_DEV, stride=COPIES), :] for j in range(COPIES)]
            send_ref[g * FACE_DEV : (g + 1) * FACE_DEV, :] = by_group(group, parts)


def first_kernel(lists_hbm, right_hbm, s0, s1, s2, s3, lists, right_ref, packed_ref, sems):
    copies = [
        pltpu.make_async_copy(lists_hbm, lists, sems.at[0]),
        pltpu.make_async_copy(right_hbm, right_ref, sems.at[1]),
    ]
    for copy in copies:
        copy.start()
    copies[1].wait()
    for t in range(DOF // COPIES):
        packed_ref[pl.ds(t, FACE_DEV, stride=FACE_DEV), :] = right_ref[:, t * LANES : (t + 1) * LANES]
    copies[0].wait()
    for direction, send_ref in zip(first_directions(), (s0, s1, s2, s3)):
        for g in range(GHOST):
            start = pl.multiple_of(lists[direction, g] * FACE_DEV, FACE_DEV)
            send_ref[g * FACE_DEV : (g + 1) * FACE_DEV, :] = packed_ref[pl.ds(start, FACE_DEV), :]


def weights_kernel(columns_any, lists_any, tiles_ref, right_ref, own_ref, ghost_ref, field_ref, columns, lists, sems):
    copies = [
        pltpu.make_async_copy(columns_any, columns, sems.at[0]),
        pltpu.make_async_copy(lists_any, lists, sems.at[1]),
    ]
    for copy in copies:
        copy.start()
    for t in range(DOF // COPIES):
        parts = spread(right_ref[:, t * LANES : (t + 1) * LANES])
        for j in range(COPIES):
            field_ref[pl.ds(COPIES * t + j, FACE_DEV, stride=DOF), :] = parts[j]
    rows = LANES // 8
    left = lax.broadcasted_iota(jnp.int32, (rows, LANES), 1) < DOF
    zero = jnp.zeros((rows, LANES), F32)
    order = list(range(OWNED)) + [None] + list(range(OWNED, BLOCKS))

    def chunk(i, carry):
        at = pl.ds(pl.multiple_of(lax.rem(i, 2) * rows, rows), rows)
        for face in range(8):
            tiles = [zero if k is None else tiles_ref[k, pl.ds(i * LANES + face, rows, stride=8), :] for k in order]
            turned = [zero if k is None else pltpu.roll(tile, DOF, 1) for k, tile in zip(order, tiles)]
            number = lax.div(i, 2) * 8 + face
            for q in range(len(order) // 2):
                even = jnp.where(left, tiles[2 * q], turned[2 * q + 1])
                odd = jnp.where(left, turned[2 * q], tiles[2 * q + 1])
                if q < OWN_DEPTH // LANES:
                    ref, lane = own_ref, q * LANES
                else:
                    ref, lane = ghost_ref, q * LANES - OWN_DEPTH
                for s, part in ((0, even), (1, odd)):
                    high = part.astype(BF16)
                    ref[number, s, at, lane : lane + LANES] = high
                    ref[number, 2 + s, at, lane : lane + LANES] = (part - high.astype(F32)).astype(BF16)
        return carry

    lax.fori_loop(0, CHUNKS, chunk, 0)
    for copy in copies:
        copy.wait()


def product(weights_ref, face, picked):
    weights = weights_ref[face].reshape(2 * DOF, picked.shape[0])
    both = jnp.dot(weights, picked, preferred_element_type=F32)
    both = both[:DOF] + both[DOF:]
    return both + pltpu.roll(both, NRHS, 1)


def pick(rows_ref, numbers):
    starts = [pl.multiple_of(number * DOF, DOF) for number in numbers]
    return jnp.concatenate([rows_ref[pl.ds(start, DOF), :] for start in starts], axis=0)


def own_kernel(columns, field_ref, weights_ref, sum_ref, split_ref):
    for face in range(FACE_DEV):
        at = slice(face * DOF, (face + 1) * DOF)
        split_ref[at, :] = high_low(field_ref[at, :])
    for face in range(FACE_DEV):
        numbers = [columns[face, k] for k in range(OWNED)]
        picked = pick(split_ref, numbers + numbers[:1])
        sum_ref[face * DOF : (face + 1) * DOF, :] = product(weights_ref, face, picked)


def add_ghosts(columns, received, sum_ref, weights_ref, field_ref, spread_ref, split_ref):
    for direction, received_ref in zip(first_directions(), received):
        keep = inside(direction)
        for g in range(GHOST):
            tile = received_ref[g * FACE_DEV : (g + 1) * FACE_DEV, :]
            parts = spread(jnp.where(keep, tile, 0.0))
            start = (direction * GHOST + g) * DOF
            for j in range(COPIES):
                spread_ref[pl.ds(start + j, FACE_DEV, stride=COPIES), :] = parts[j]
    for slot in range(4 * GHOST):
        at = slice(slot * DOF, (slot + 1) * DOF)
        split_ref[at, :] = high_low(spread_ref[at, :])
    for face in range(FACE_DEV):
        picked = pick(split_ref, [columns[face, k] - FACE_DEV for k in range(OWNED, BLOCKS)])
        total = sum_ref[face * DOF : (face + 1) * DOF, :] + product(weights_ref, face, picked)
        for s in range(2):
            rows = pl.ds(face * DOF + s, DOF // 2, stride=2)
            field_ref[rows, :] = total[s * DOF // 2 : (s + 1) * DOF // 2, :]


def ghost_kernel(columns, lists, r0, r1, r2, r3, sum_ref, weights_ref, field_ref, s0, s1, s2, s3, spread_ref, split_ref):
    add_ghosts(columns, (r0, r1, r2, r3), sum_ref, weights_ref, field_ref, spread_ref, split_ref)
    write_sends(lists, field_ref, (s0, s1, s2, s3))


def last_kernel(
    columns, r0, r1, r2, r3, sum_ref, weights_ref, f0, f1, f2, system_ref, basis_ref, f3, spread_ref, split_ref
):
    add_ghosts(columns, (r0, r1, r2, r3), sum_ref, weights_ref, f3, spread_ref, split_ref)
    group = lane_group(LANES)
    gram = jnp.zeros((LANES, 2 * LANES), F32)
    for part in range(ROWS // LANES):
        at = slice(part * LANES, (part + 1) * LANES)
        basis = by_group(group, [ref[at, :] for ref in (f0, f1, f2, f3)])
        high = basis.astype(BF16)
        low = (basis - high.astype(F32)).astype(BF16)
        both = jnp.concatenate([high, low], axis=1)
        basis_ref[at, :] = both
        gram = gram + lax.dot_general(high, both, (((0,), (0,)), ((), ())), preferred_element_type=F32)
    cross = gram[:, LANES:]
    full = gram[:, :LANES] + cross + cross.T
    pairs = full[:SYSTEM] + full[NRHS:]
    lane = lax.broadcasted_iota(jnp.int32, (SYSTEM, LANES), 1)
    system_ref[...] = pltpu.roll(pairs, SYSTEM, 1) + jnp.where(lane < SYSTEM, pairs, 0.0)


def eliminate(system):
    row = lax.broadcasted_iota(jnp.int32, (SYSTEM, LANES), 0)
    count = range(PIVOTS)
    for j in range(0, SYSTEM, PIVOTS):
        lines = [system[j + i : j + i + 1, :] for i in count]
        block = [[jnp.broadcast_to(lines[k][:, j + i : j + i + 1], (1, LANES)) for k in range(i + 1)] for i in count]
        inverse = [None] * PIVOTS
        lower = [[None] * PIVOTS for _ in count]
        for k in count:
            inverse[k] = 1.0 / block[k][k]
            for i in range(k + 1, PIVOTS):
                lower[i][k] = block[i][k] * inverse[k]
            for i in range(k + 1, PIVOTS):
                for q in range(k + 1, i + 1):
                    block[i][q] = block[i][q] - lower[i][k] * block[q][k]
        solved = list(lines)
        for k in count:
            for i in range(k + 1, PIVOTS):
                solved[i] = solved[i] - lower[i][k] * solved[k]
        solved = [solved[i] * inverse[i] for i in count]
        for k in reversed(count):
            for i in range(k):
                solved[i] = solved[i] - lower[k][i] * solved[k]
        factors = [system[:, j + i : j + i + 1] for i in count]
        for i in count:
            system = system - factors[i] * solved[i]
        for i in count:
            system = jnp.where(row == j + i, solved[i], system)
    return system


def finish_kernel(mine, other, basis_ref, solution_hbm, residual_hbm, out_ref, result_ref, sems):
    system = eliminate(mine[...] + other[...])
    lane = lax.broadcasted_iota(jnp.int32, (SYSTEM, LANES), 1)
    coeffs = jnp.where(lane >= SYSTEM, system, 0.0)
    coeffs = coeffs + pltpu.roll(coeffs, NRHS, 1)
    coeffs = coeffs + pltpu.roll(coeffs, 2 * NRHS, 1)
    zero = jnp.zeros((NRHS, LANES), F32)
    first_row = lax.broadcasted_iota(jnp.int32, (LANES, LANES), 0)
    first_lane = lax.broadcasted_iota(jnp.int32, (LANES, LANES), 1)
    first = jnp.where(first_row == first_lane % NRHS, 1.0, 0.0)
    padded = jnp.concatenate([coeffs, zero], axis=0)
    combo = first - (padded + jnp.concatenate([zero, coeffs], axis=0))
    both = jnp.concatenate([padded, combo], axis=1)
    high = both.astype(BF16)
    low = (both - high.astype(F32)).astype(BF16)
    twice = jnp.concatenate([high, high], axis=0)
    for part in range(ROWS // LANES):
        at = slice(part * LANES, (part + 1) * LANES)
        out = jnp.dot(basis_ref[at, :], twice, preferred_element_type=F32)
        out = out + jnp.dot(basis_ref[at, :LANES], low, preferred_element_type=F32)
        out_ref[0, at, :] = out[:, :LANES]
        out_ref[1, at, :] = out[:, LANES:]
    group = lane_group(FACE_DEV)
    copies = []
    for side, result_hbm in ((0, solution_hbm), (1, residual_hbm)):
        for t in range(DOF // COPIES):
            parts = [out_ref[side, pl.ds(COPIES * t + j, FACE_DEV, stride=DOF), :] for j in range(COPIES)]
            result_ref[side, :, t * LANES : (t + 1) * LANES] = by_group(group, parts)
        copies.append(pltpu.make_async_copy(result_ref.at[side], result_hbm, sems.at[side]))
        copies[side].start()
    for copy in copies:
        copy.wait()


def pairs_of(size, second):
    if not second:
        return [(i, i ^ 1) for i in range(size)]
    ahead = [(i, (i + 1) % size) for i in range(1, size, 2)]
    return ahead + [(b, a) for a, b in ahead]


def exchange(sends):
    routes = (("fx", True), ("fx", False), ("fy", True), ("fy", False))
    return [
        lax.ppermute(send, axis, pairs_of(lax.axis_size(axis), second))
        for send, (axis, second) in zip(sends, routes)
    ]


ROUNDS = (("fy", (1,)), ("fy", (2, 6, 4)), ("fx", (1, 3, 2)), ("fx", (4, 24, 28)))
LAST_ROUND = ("fx", 8)


def from_partner(part, axis, distance):
    return lax.ppermute(part, axis, [(i, i ^ distance) for i in range(lax.axis_size(axis))])


def add_over_devices(part):
    for axis, distances in ROUNDS:
        others = [from_partner(part, axis, d) for d in distances]
        part = part + others[0]
        if len(others) == 3:
            part = part + (others[1] + others[2])
    return part, from_partner(part, *LAST_ROUND)


def in_hbm(array):
    return pltpu.with_memory_space_constraint(array, pltpu.HBM)


def params():
    return dict(compiler_params=pltpu.CompilerParams(vmem_limit_bytes=32 << 20))


def on_device(right_side, coupling, face_columns, ghost_lists):
    send = shape_of(GHOST * FACE_DEV, LANES)
    field_shape = shape_of(ROWS, LANES)
    sends = pl.pallas_call(
        first_kernel,
        out_shape=[send] * 4,
        in_specs=[HBM, HBM],
        out_specs=[VMEM] * 4,
        scratch_shapes=[
            pltpu.SMEM((4, GHOST), jnp.int32),
            pltpu.VMEM((FACE_DEV, DOF * NRHS), F32),
            pltpu.VMEM((FACE_DEV * FACE_DEV, LANES), F32),
            pltpu.SemaphoreType.DMA((2,)),
        ],
        cost_estimate=pl.CostEstimate(flops=1 << 33, transcendentals=0, bytes_accessed=16 << 20),
        name="first",
        **params(),
    )(in_hbm(ghost_lists), in_hbm(right_side))

    tiles = jnp.transpose(coupling, (1, 0, 2)).reshape(BLOCKS, 2, 8, DOF // 2, LANES)
    tiles = jnp.transpose(tiles, (0, 1, 3, 2, 4)).reshape(BLOCKS, CHUNKS * LANES, LANES)
    own_weights, ghost_weights, field, columns, lists = pl.pallas_call(
        weights_kernel,
        out_shape=[
            jax.ShapeDtypeStruct((FACE_DEV, 4, DOF // 2, OWN_DEPTH), BF16),
            jax.ShapeDtypeStruct((FACE_DEV, 4, DOF // 2, GHOST_DEPTH), BF16),
            field_shape,
            pltpu.SMEM((FACE_DEV, BLOCKS), jnp.int32),
            pltpu.SMEM((4, GHOST), jnp.int32),
        ],
        in_specs=[ANY, ANY, VMEM, VMEM],
        out_specs=[VMEM] * 3 + [SMEM] * 2,
        scratch_shapes=[pltpu.SemaphoreType.DMA((2,))],
        cost_estimate=pl.CostEstimate(flops=0, transcendentals=0, bytes_accessed=6 << 20),
        name="weights",
        **params(),
    )(face_columns, ghost_lists, tiles, right_side)
    fields = [field]

    own_call = pl.pallas_call(
        own_kernel,
        out_shape=field_shape,
        in_specs=[SMEM, VMEM, VMEM],
        out_specs=VMEM,
        scratch_shapes=[pltpu.VMEM((ROWS, LANES), BF16)],
        cost_estimate=pl.CostEstimate(flops=1 << 30, transcendentals=0, bytes_accessed=3 << 20),
        name="own",
        **params(),
    )
    scratch = [
        pltpu.VMEM((4 * GHOST * DOF, LANES), F32),
        pltpu.VMEM((4 * GHOST * DOF, LANES), BF16),
    ]
    ghost_call = pl.pallas_call(
        ghost_kernel,
        out_shape=[field_shape] + [send] * 4,
        in_specs=[SMEM, SMEM] + [VMEM] * 6,
        out_specs=[VMEM] * 5,
        scratch_shapes=scratch,
        name="ghost",
        **params(),
    )
    last_call = pl.pallas_call(
        last_kernel,
        out_shape=[shape_of(SYSTEM, LANES), shape_of(ROWS, 2 * LANES, BF16)],
        in_specs=[SMEM] + [VMEM] * 9,
        out_specs=[VMEM] * 2,
        scratch_shapes=[pltpu.VMEM((ROWS, LANES), F32)] + scratch,
        name="last",
        **params(),
    )
    columns = pltpu.with_memory_space_constraint(columns, pltpu.SMEM)
    lists = pltpu.with_memory_space_constraint(lists, pltpu.SMEM)
    for power in range(POWERS):
        received = exchange(sends)
        own_sum = own_call(columns, fields[-1], own_weights)
        if power < POWERS - 1:
            outs = ghost_call(columns, lists, *received, own_sum, ghost_weights)
            fields.append(outs[0])
            sends = outs[1:]
        else:
            system, basis = last_call(columns, *received, own_sum, ghost_weights, *fields)
    mine, other = add_over_devices(system)
    result = shape_of(FACE_DEV, DOF * NRHS)
    return tuple(
        pl.pallas_call(
            finish_kernel,
            out_shape=[result, result],
            in_specs=[VMEM] * 3,
            out_specs=[HBM] * 2,
            scratch_shapes=[
                pltpu.VMEM((2, ROWS, LANES), F32),
                pltpu.VMEM((2, FACE_DEV, DOF * NRHS), F32),
                pltpu.SemaphoreType.DMA((2,)),
            ],
            name="finish",
            **params(),
        )(mine, other, basis)
    )


def solution(mesh):
    placed = (
        P(("fx", "fy"), None),
        P(("fx", "fy"), None, None),
        P(("fx", "fy"), None),
        P(("fx", "fy"), None),
    )
    return jax.shard_map(
        on_device,
        mesh=mesh,
        in_specs=placed,
        out_specs=(P(("fx", "fy"), None), P(("fx", "fy"), None)),
        check_vma=False,
    )
```

```python
import functools

import jax
import jax.numpy as jnp
from jax import lax
from jax.experimental import pallas as pl
from jax.experimental.pallas import tpu as pltpu
from jax.sharding import PartitionSpec as P

DOF = 64
NRHS = 32
BLOCKS = 11
OWNED = 7
POWERS = 3
FACE_DEV = 16
GHOST = 4
LANES = 128
COPIES = LANES // NRHS
ROWS = FACE_DEV * DOF
OWN_DEPTH = 512
GHOST_DEPTH = 256
SYSTEM = POWERS * NRHS
PACKED = 9 * NRHS * NRHS // LANES
CHUNKS = 4
PIVOTS = 8

VMEM = pl.BlockSpec(memory_space=pltpu.VMEM)
ANY = pl.BlockSpec(memory_space=pl.ANY)
SMEM = pl.BlockSpec(memory_space=pltpu.SMEM)
HBM = pl.BlockSpec(memory_space=pltpu.HBM)
F32 = jnp.float32
BF16 = jnp.bfloat16


def shape_of(rows, columns, dtype=F32):
    return jax.ShapeDtypeStruct((rows, columns), dtype)


def lane_group(rows):
    return lax.broadcasted_iota(jnp.int32, (rows, LANES), 1) // NRHS


def by_group(group, parts):
    low = jnp.where(group == 0, parts[0], parts[1])
    high = jnp.where(group == 2, parts[2], parts[3])
    return jnp.where(group < 2, low, high)


def spread(tile):
    group = lane_group(tile.shape[0])
    turned = [tile] + [pltpu.roll(tile, NRHS * s, 1) for s in range(1, COPIES)]
    return [by_group(group, [turned[(c - j) % COPIES] for c in range(COPIES)]) for j in range(COPIES)]


def high_low(field):
    group = lane_group(field.shape[0])
    high = field.astype(BF16).astype(F32)
    return jnp.where(group % 2 == 0, high, field - high).astype(BF16)


def first_directions():
    odd_x = lax.rem(lax.axis_index("fx"), 2)
    odd_y = lax.rem(lax.axis_index("fy"), 2)
    return (odd_x, 2 + odd_y, 1 - odd_x, 3 - odd_y)


def inside(direction):
    fx, fy = lax.axis_index("fx"), lax.axis_index("fy")
    last_x, last_y = lax.axis_size("fx") - 1, lax.axis_size("fy") - 1
    out = (direction == 0) & (fx == 0) | (direction == 1) & (fx == last_x)
    return jnp.logical_not(out | (direction == 2) & (fy == 0) | (direction == 3) & (fy == last_y))


def write_sends(lists, field_ref, send_refs):
    group = lane_group(FACE_DEV)
    for direction, send_ref in zip(first_directions(), send_refs):
        for g in range(GHOST):
            start = lists[direction, g] * DOF
            parts = [field_ref[pl.ds(start + j, FACE_DEV, stride=COPIES), :] for j in range(COPIES)]
            send_ref[g * FACE_DEV : (g + 1) * FACE_DEV, :] = by_group(group, parts)


def first_kernel(lists_hbm, right_hbm, s0, s1, s2, s3, lists, right_ref, packed_ref, sems):
    copies = [
        pltpu.make_async_copy(lists_hbm, lists, sems.at[0]),
        pltpu.make_async_copy(right_hbm, right_ref, sems.at[1]),
    ]
    for copy in copies:
        copy.start()
    copies[1].wait()
    for t in range(DOF // COPIES):
        packed_ref[pl.ds(t, FACE_DEV, stride=FACE_DEV), :] = right_ref[:, t * LANES : (t + 1) * LANES]
    copies[0].wait()
    for direction, send_ref in zip(first_directions(), (s0, s1, s2, s3)):
        for g in range(GHOST):
            start = pl.multiple_of(lists[direction, g] * FACE_DEV, FACE_DEV)
            send_ref[g * FACE_DEV : (g + 1) * FACE_DEV, :] = packed_ref[pl.ds(start, FACE_DEV), :]


def weights_kernel(columns_any, lists_any, tiles_ref, right_ref, own_ref, ghost_ref, field_ref, columns, lists, sems):
    copies = [
        pltpu.make_async_copy(columns_any, columns, sems.at[0]),
        pltpu.make_async_copy(lists_any, lists, sems.at[1]),
    ]
    for copy in copies:
        copy.start()
    for t in range(DOF // COPIES):
        parts = spread(right_ref[:, t * LANES : (t + 1) * LANES])
        for j in range(COPIES):
            field_ref[pl.ds(COPIES * t + j, FACE_DEV, stride=DOF), :] = parts[j]
    rows = LANES // 8
    left = lax.broadcasted_iota(jnp.int32, (rows, LANES), 1) < DOF
    zero = jnp.zeros((rows, LANES), F32)
    order = list(range(OWNED)) + [None] + list(range(OWNED, BLOCKS))

    def chunk(i, carry):
        at = pl.ds(pl.multiple_of(lax.rem(i, 2) * rows, rows), rows)
        for face in range(8):
            tiles = [zero if k is None else tiles_ref[k, pl.ds(i * LANES + face, rows, stride=8), :] for k in order]
            number = lax.div(i, 2) * 8 + face
            for q in range(len(order) // 2):
                one, two = tiles[2 * q : 2 * q + 2]
                moved = pltpu.roll(jnp.where(left, two, one), DOF, 1)
                even = jnp.where(left, one, moved)
                odd = jnp.where(left, moved, two)
                if q < OWN_DEPTH // LANES:
                    ref, lane = own_ref, q * LANES
                else:
                    ref, lane = ghost_ref, q * LANES - OWN_DEPTH
                for s, part in ((0, even), (1, odd)):
                    high = part.astype(BF16)
                    ref[number, s, at, lane : lane + LANES] = high
                    ref[number, 2 + s, at, lane : lane + LANES] = (part - high.astype(F32)).astype(BF16)
        return carry

    lax.fori_loop(0, CHUNKS, chunk, 0)
    for copy in copies:
        copy.wait()


def product(weights_ref, face, picked):
    weights = weights_ref[face].reshape(2 * DOF, picked.shape[0])
    both = jnp.dot(weights, picked, preferred_element_type=F32)
    both = both[:DOF] + both[DOF:]
    return both + pltpu.roll(both, NRHS, 1)


def pick(rows_ref, numbers):
    starts = [pl.multiple_of(number * DOF, DOF) for number in numbers]
    return jnp.concatenate([rows_ref[pl.ds(start, DOF), :] for start in starts], axis=0)


def own_kernel(columns, field_ref, weights_ref, sum_ref, split_ref):
    for face in range(FACE_DEV):
        at = slice(face * DOF, (face + 1) * DOF)
        split_ref[at, :] = high_low(field_ref[at, :])
    for face in range(FACE_DEV):
        numbers = [columns[face, k] for k in range(OWNED)]
        picked = pick(split_ref, numbers + numbers[:1])
        sum_ref[face * DOF : (face + 1) * DOF, :] = product(weights_ref, face, picked)


def add_ghosts(columns, received, sum_ref, weights_ref, field_ref, spread_ref, split_ref):
    for direction, received_ref in zip(first_directions(), received):
        keep = inside(direction)
        for g in range(GHOST):
            tile = received_ref[g * FACE_DEV : (g + 1) * FACE_DEV, :]
            parts = spread(jnp.where(keep, tile, 0.0))
            start = (direction * GHOST + g) * DOF
            for j in range(COPIES):
                spread_ref[pl.ds(start + j, FACE_DEV, stride=COPIES), :] = parts[j]
    for slot in range(4 * GHOST):
        at = slice(slot * DOF, (slot + 1) * DOF)
        split_ref[at, :] = high_low(spread_ref[at, :])
    for face in range(FACE_DEV):
        picked = pick(split_ref, [columns[face, k] - FACE_DEV for k in range(OWNED, BLOCKS)])
        total = sum_ref[face * DOF : (face + 1) * DOF, :] + product(weights_ref, face, picked)
        for s in range(2):
            rows = pl.ds(face * DOF + s, DOF // 2, stride=2)
            field_ref[rows, :] = total[s * DOF // 2 : (s + 1) * DOF // 2, :]


def ghost_kernel(columns, lists, r0, r1, r2, r3, sum_ref, weights_ref, field_ref, s0, s1, s2, s3, spread_ref, split_ref):
    add_ghosts(columns, (r0, r1, r2, r3), sum_ref, weights_ref, field_ref, spread_ref, split_ref)
    write_sends(lists, field_ref, (s0, s1, s2, s3))


def pack(system):
    lane = lax.broadcasted_iota(jnp.int32, (NRHS, LANES), 1)
    bottom = system[2 * NRHS :]
    middle = jnp.where(lane < NRHS, pltpu.roll(bottom, 2 * NRHS, 1), system[NRHS : 2 * NRHS])
    pieces = [pltpu.roll(bottom[8 * i : 8 * i + 8], NRHS * (i + 1) % LANES, 1) if i < 3 else bottom[24:] for i in range(4)]
    return jnp.concatenate([system[:NRHS], middle, by_group(lane_group(8), pieces)], axis=0)


def unpack(packed):
    lane = lax.broadcasted_iota(jnp.int32, (NRHS, LANES), 1)
    middle, tail = packed[NRHS : 2 * NRHS], packed[2 * NRHS :]
    terms = [pltpu.roll(tail, NRHS * (3 - i), 1) if i < 3 else tail for i in range(4)]
    bottom = jnp.where(lane < SYSTEM, pltpu.roll(middle, 2 * NRHS, 1), jnp.concatenate(terms, axis=0))
    upper = jnp.concatenate([packed[: 2 * NRHS], bottom, jnp.zeros((NRHS, LANES), F32)], axis=0)
    block_row = lax.broadcasted_iota(jnp.int32, (SYSTEM, LANES), 0) // NRHS
    block_lane = lax.broadcasted_iota(jnp.int32, (SYSTEM, LANES), 1) // NRHS
    return jnp.where(block_lane < block_row, upper.T[:SYSTEM], upper[:SYSTEM])


def last_kernel(
    columns, r0, r1, r2, r3, sum_ref, weights_ref, f0, f1, f2, system_ref, basis_ref, f3, spread_ref, split_ref
):
    add_ghosts(columns, (r0, r1, r2, r3), sum_ref, weights_ref, f3, spread_ref, split_ref)
    group = lane_group(LANES)
    gram = jnp.zeros((LANES, 2 * LANES), F32)
    for part in range(ROWS // LANES):
        at = slice(part * LANES, (part + 1) * LANES)
        basis = by_group(group, [ref[at, :] for ref in (f0, f1, f2, f3)])
        high = basis.astype(BF16)
        low = (basis - high.astype(F32)).astype(BF16)
        both = jnp.concatenate([high, low], axis=1)
        basis_ref[at, :] = both
        gram = gram + lax.dot_general(high, both, (((0,), (0,)), ((), ())), preferred_element_type=F32)
    cross = gram[:, LANES:]
    full = gram[:, :LANES] + cross + cross.T
    pairs = full[:SYSTEM] + full[NRHS:]
    lane = lax.broadcasted_iota(jnp.int32, (SYSTEM, LANES), 1)
    system_ref[...] = pack(pltpu.roll(pairs, SYSTEM, 1) + jnp.where(lane < SYSTEM, pairs, 0.0))


def eliminate(system):
    row = lax.broadcasted_iota(jnp.int32, (SYSTEM, LANES), 0)
    count = range(PIVOTS)
    for j in range(0, SYSTEM, PIVOTS):
        lines = [system[j + i : j + i + 1, :] for i in count]
        block = [[jnp.broadcast_to(lines[k][:, j + i : j + i + 1], (1, LANES)) for k in range(i + 1)] for i in count]
        inverse = [None] * PIVOTS
        lower = [[None] * PIVOTS for _ in count]
        for k in count:
            inverse[k] = 1.0 / block[k][k]
            for i in range(k + 1, PIVOTS):
                lower[i][k] = block[i][k] * inverse[k]
            for i in range(k + 1, PIVOTS):
                for q in range(k + 1, i + 1):
                    block[i][q] = block[i][q] - lower[i][k] * block[q][k]
        solved = list(lines)
        for k in count:
            for i in range(k + 1, PIVOTS):
                solved[i] = solved[i] - lower[i][k] * solved[k]
        solved = [solved[i] * inverse[i] for i in count]
        for k in reversed(count):
            for i in range(k):
                solved[i] = solved[i] - lower[k][i] * solved[k]
        factors = [system[:, j + i : j + i + 1] for i in count]
        for i in count:
            system = system - factors[i] * solved[i]
        for i in count:
            system = jnp.where(row == j + i, solved[i], system)
    return system


def finish_kernel(mine, other, basis_ref, solution_hbm, residual_hbm, out_ref, result_ref, sems):
    system = eliminate(unpack(mine[...] + other[...]))
    lane = lax.broadcasted_iota(jnp.int32, (SYSTEM, LANES), 1)
    coeffs = jnp.where(lane >= SYSTEM, system, 0.0)
    coeffs = coeffs + pltpu.roll(coeffs, NRHS, 1)
    coeffs = coeffs + pltpu.roll(coeffs, 2 * NRHS, 1)
    zero = jnp.zeros((NRHS, LANES), F32)
    first_row = lax.broadcasted_iota(jnp.int32, (LANES, LANES), 0)
    first_lane = lax.broadcasted_iota(jnp.int32, (LANES, LANES), 1)
    first = jnp.where(first_row == first_lane % NRHS, 1.0, 0.0)
    padded = jnp.concatenate([coeffs, zero], axis=0)
    combo = first - (padded + jnp.concatenate([zero, coeffs], axis=0))
    both = jnp.concatenate([padded, combo], axis=1)
    high = both.astype(BF16)
    low = (both - high.astype(F32)).astype(BF16)
    twice = jnp.concatenate([high, high], axis=0)
    for part in range(ROWS // LANES):
        at = slice(part * LANES, (part + 1) * LANES)
        out = jnp.dot(basis_ref[at, :], twice, preferred_element_type=F32)
        out = out + jnp.dot(basis_ref[at, :LANES], low, preferred_element_type=F32)
        out_ref[0, at, :] = out[:, :LANES]
        out_ref[1, at, :] = out[:, LANES:]
    group = lane_group(FACE_DEV)
    copies = []
    for side, result_hbm in ((0, solution_hbm), (1, residual_hbm)):
        for t in range(DOF // COPIES):
            parts = [out_ref[side, pl.ds(COPIES * t + j, FACE_DEV, stride=DOF), :] for j in range(COPIES)]
            result_ref[side, :, t * LANES : (t + 1) * LANES] = by_group(group, parts)
        copies.append(pltpu.make_async_copy(result_ref.at[side], result_hbm, sems.at[side]))
        copies[side].start()
    for copy in copies:
        copy.wait()


def pairs_of(size, second):
    if not second:
        return [(i, i ^ 1) for i in range(size)]
    ahead = [(i, (i + 1) % size) for i in range(1, size, 2)]
    return ahead + [(b, a) for a, b in ahead]


def exchange(sends):
    routes = (("fx", True), ("fy", True), ("fx", False), ("fy", False))
    return [
        lax.ppermute(send, axis, pairs_of(lax.axis_size(axis), second))
        for send, (axis, second) in zip(sends, routes)
    ]


ROUNDS = (("fy", (1,)), ("fy", (2, 6, 4)), ("fx", (1, 3, 2)), ("fx", (4, 24, 28)))
LAST_ROUND = ("fx", 8)


def from_partner(part, axis, distance):
    return lax.ppermute(part, axis, [(i, i ^ distance) for i in range(lax.axis_size(axis))])


def add_over_devices(part):
    for axis, distances in ROUNDS:
        others = [from_partner(part, axis, d) for d in distances]
        part = part + others[0]
        if len(others) == 3:
            part = part + (others[1] + others[2])
    return part, from_partner(part, *LAST_ROUND)


def in_hbm(array):
    return pltpu.with_memory_space_constraint(array, pltpu.HBM)


def params():
    return dict(compiler_params=pltpu.CompilerParams(vmem_limit_bytes=32 << 20))


def on_device(right_side, coupling, face_columns, ghost_lists):
    send = shape_of(GHOST * FACE_DEV, LANES)
    field_shape = shape_of(ROWS, LANES)
    sends = pl.pallas_call(
        first_kernel,
        out_shape=[send] * 4,
        in_specs=[HBM, HBM],
        out_specs=[VMEM] * 4,
        scratch_shapes=[
            pltpu.SMEM((4, GHOST), jnp.int32),
            pltpu.VMEM((FACE_DEV, DOF * NRHS), F32),
            pltpu.VMEM((FACE_DEV * FACE_DEV, LANES), F32),
            pltpu.SemaphoreType.DMA((2,)),
        ],
        cost_estimate=pl.CostEstimate(flops=1 << 33, transcendentals=0, bytes_accessed=16 << 20),
        name="first",
        **params(),
    )(in_hbm(ghost_lists), in_hbm(right_side))

    tiles = jnp.transpose(coupling, (1, 0, 2)).reshape(BLOCKS, 2, 8, DOF // 2, LANES)
    tiles = jnp.transpose(tiles, (0, 1, 3, 2, 4)).reshape(BLOCKS, CHUNKS * LANES, LANES)
    own_weights, ghost_weights, field, columns, lists = pl.pallas_call(
        weights_kernel,
        out_shape=[
            jax.ShapeDtypeStruct((FACE_DEV, 4, DOF // 2, OWN_DEPTH), BF16),
            jax.ShapeDtypeStruct((FACE_DEV, 4, DOF // 2, GHOST_DEPTH), BF16),
            field_shape,
            pltpu.SMEM((FACE_DEV, BLOCKS), jnp.int32),
            pltpu.SMEM((4, GHOST), jnp.int32),
        ],
        in_specs=[ANY, ANY, VMEM, VMEM],
        out_specs=[VMEM] * 3 + [SMEM] * 2,
        scratch_shapes=[pltpu.SemaphoreType.DMA((2,))],
        cost_estimate=pl.CostEstimate(flops=0, transcendentals=0, bytes_accessed=6 << 20),
        name="weights",
        **params(),
    )(face_columns, ghost_lists, tiles, right_side)
    fields = [field]

    own_call = pl.pallas_call(
        own_kernel,
        out_shape=field_shape,
        in_specs=[SMEM, VMEM, VMEM],
        out_specs=VMEM,
        scratch_shapes=[pltpu.VMEM((ROWS, LANES), BF16)],
        cost_estimate=pl.CostEstimate(flops=1 << 30, transcendentals=0, bytes_accessed=3 << 20),
        name="own",
        **params(),
    )
    scratch = [
        pltpu.VMEM((4 * GHOST * DOF, LANES), F32),
        pltpu.VMEM((4 * GHOST * DOF, LANES), BF16),
    ]
    ghost_call = pl.pallas_call(
        ghost_kernel,
        out_shape=[field_shape] + [send] * 4,
        in_specs=[SMEM, SMEM] + [VMEM] * 6,
        out_specs=[VMEM] * 5,
        scratch_shapes=scratch,
        name="ghost",
        **params(),
    )
    last_call = pl.pallas_call(
        last_kernel,
        out_shape=[shape_of(PACKED, LANES), shape_of(ROWS, 2 * LANES, BF16)],
        in_specs=[SMEM] + [VMEM] * 9,
        out_specs=[VMEM] * 2,
        scratch_shapes=[pltpu.VMEM((ROWS, LANES), F32)] + scratch,
        name="last",
        **params(),
    )
    columns = pltpu.with_memory_space_constraint(columns, pltpu.SMEM)
    lists = pltpu.with_memory_space_constraint(lists, pltpu.SMEM)
    for power in range(POWERS):
        received = exchange(sends)
        own_sum = own_call(columns, fields[-1], own_weights)
        if power < POWERS - 1:
            outs = ghost_call(columns, lists, *received, own_sum, ghost_weights)
            fields.append(outs[0])
            sends = outs[1:]
        else:
            system, basis = last_call(columns, *received, own_sum, ghost_weights, *fields)
    mine, other = add_over_devices(system)
    result = shape_of(FACE_DEV, DOF * NRHS)
    return tuple(
        pl.pallas_call(
            finish_kernel,
            out_shape=[result, result],
            in_specs=[VMEM] * 3,
            out_specs=[HBM] * 2,
            scratch_shapes=[
                pltpu.VMEM((2, ROWS, LANES), F32),
                pltpu.VMEM((2, FACE_DEV, DOF * NRHS), F32),
                pltpu.SemaphoreType.DMA((2,)),
            ],
            name="finish",
            **params(),
        )(mine, other, basis)
    )


def solution(mesh):
    placed = (
        P(("fx", "fy"), None),
        P(("fx", "fy"), None, None),
        P(("fx", "fy"), None),
        P(("fx", "fy"), None),
    )
    return jax.shard_map(
        on_device,
        mesh=mesh,
        in_specs=placed,
        out_specs=(P(("fx", "fy"), None), P(("fx", "fy"), None)),
        check_vma=False,
    )
```
